32 devices in a mesh: pipe: 16 (over z, y, core), tensor: 2 (over x).
Axes of the slice: x: 2, y: 2, z: 4, core: 2. Of those that a mesh axis runs over, the one named last changes fastest.
Arguments:
- tokens_x: bfloat16 [16, 384, 12288], P('pipe', None, 'tensor'), may hold values from -6 to 6
- queries: bfloat16 [16, 384, 12288], P('pipe', None, 'tensor'), may hold values from -120 to 120
- key_rows: bfloat16 [16, 384, 1024], P('pipe', None, 'tensor'), may hold values from -5 to 5
- out_grad: bfloat16 [16, 384, 12288], P('pipe', None, 'tensor'), may hold values from -4 to 4
- value_weight: bfloat16 [16, 12288, 1024], P('pipe', 'tensor'), may hold values from -0.0546875 to 0.0546875
- doc_starts: int32 [16, 384], P('pipe'), may hold values from 0 to 383, as said below
Outputs:
- query_grad: bfloat16 [16, 384, 12288], P('pipe', None, 'tensor')
- key_grad: bfloat16 [16, 384, 1024], P('pipe', None, 'tensor')
- weight_grad: bfloat16 [16, 12288, 1024], P('pipe', 'tensor')
- section_grad: bfloat16 [16, 384, 12288], P('pipe', None, 'tensor')
The draws below stay inside these ranges and needn't reach their ends.
Inputs may be any that keep to these rules, and one draw needn't show every extreme that they name: doc_starts[s, 0] = 0, doc_starts[s, 383] = 383, doc_starts[s, i] <= i, and doc_starts[s, i] is either doc_starts[s, i - 1] or i.
All inputs are finite; a program needn't handle non-finite values.
Results may differ from the reference program's by a relative error of at most 0.012.
The reference program's roundings to bfloat16 on the way count: a program that leaves them out, or rounds other values in their place, can miss the bound.
Values may be sent and summed in bfloat16 or wider, within the bound.
A program may use at most 256 MiB of HBM per device.

```python
import jax
import jax.numpy as jnp
from jax import lax

D = 12288
HQ = 96
KV = 8
HD = 128
TOK = 384
SECTIONS = 16


def paired_draw(key):
    base = jax.random.fold_in(key, 101)
    key_k, key_q = jax.random.split(base, 2)
    keys_all = jnp.clip(jax.random.normal(key_k, (SECTIONS, TOK, KV, HD), jnp.float32), -5.0, 5.0)
    queries_all = jnp.clip(jax.random.normal(key_q, (SECTIONS, TOK, KV, HQ // KV, HD), jnp.float32), -5.0, 5.0)
    return (queries_all.reshape(SECTIONS, TOK, HQ * HD), keys_all.reshape(SECTIONS, TOK, KV * HD))


def draw_queries(key, part):
    return paired_draw(key)[0].astype(jnp.bfloat16)


def draw_key_rows(key, part):
    return paired_draw(key)[1].astype(jnp.bfloat16)


def draw_doc_starts(key, part):
    flags = jax.random.randint(jax.random.fold_in(key, 202), (SECTIONS, TOK), 0, 48) == 0
    position = jnp.arange(TOK, dtype=jnp.int32)[None, :]
    marked = jnp.where(flags | (position == 0) | (position == TOK - 1), position, 0).astype(jnp.int32)
    return lax.cummax(marked, axis=1).astype(jnp.int32)


def steps_of(rng, extent, cuts, least, high):
    gain = 1.0
    for axis_at, parts in cuts:
        steps = jax.random.uniform(jax.random.fold_in(jax.random.fold_in(rng, 6), axis_at), (parts,), jnp.float32, least / len(cuts), high / len(cuts))
        gain = gain * jnp.repeat(jnp.exp(steps), extent[axis_at] // parts).reshape((-1,) + (1,) * (len(extent) - 1 - axis_at))
    return gain


def normal_values(key, shape, width, bound, cuts=(), held_as=jnp.bfloat16):
    drawn = width * jax.random.normal(key, shape, jnp.float32)
    if cuts:
        drawn = drawn * steps_of(key, shape, cuts, -0.22, 0.18)
    return jnp.clip(drawn, -bound, bound).astype(held_as)


def setup_inputs(seed: int = 0) -> dict:
    key_of = jax.random.split(jax.random.key(seed), 7)
    tokens_x = normal_values(key_of[0], (SECTIONS, TOK, D), 1.0, 6.0, ((0, 16), (2, 2)))
    queries = draw_queries(jax.random.fold_in(key_of[6], 71), 0)
    key_rows = draw_key_rows(jax.random.fold_in(key_of[6], 71), 0)
    out_grad = normal_values(key_of[3], (SECTIONS, TOK, HQ * HD), 0.25, 4.0, ((0, 16), (2, 2)))
    value_weight = normal_values(key_of[4], (SECTIONS, D, KV * HD), D ** -0.5, 0.0546875, ((0, 16), (1, 2)))
    doc_starts = draw_doc_starts(jax.random.fold_in(key_of[6], 71), 0)
    return dict(tokens_x=tokens_x, queries=queries, key_rows=key_rows, out_grad=out_grad, value_weight=value_weight, doc_starts=doc_starts)


def attend(queries, key_rows, values, out_grad, doc_starts):
    length = queries.shape[0]
    kv_heads = key_rows.shape[1] // HD
    groups = queries.shape[1] // (kv_heads * HD)
    scaling = HD ** -0.5
    row_index = lax.broadcasted_iota(jnp.int32, (length, length), 0)
    col_index = lax.broadcasted_iota(jnp.int32, (length, length), 1)
    allowed = (col_index <= row_index) & (col_index >= doc_starts[:, None])
    query_heads = queries.reshape(length, kv_heads, groups, HD)
    key_heads = key_rows.reshape(length, kv_heads, HD)
    value_heads = values.reshape(length, kv_heads, HD)
    grad_heads = out_grad.reshape(length, kv_heads, groups, HD)

    def one_group(query_g, key_g, value_g, grad_g):
        query_f = query_g.astype(jnp.float32)
        key_f = key_g.astype(jnp.float32)
        value_f = value_g.astype(jnp.float32)
        grad_f = grad_g.astype(jnp.float32)
        scores = jnp.einsum("igd,jd->gij", query_f, key_f) * scaling
        scores = jnp.where(allowed[None], scores, -1e30)
        top_score = jnp.max(scores, axis=2, keepdims=True)
        expo = jnp.exp(scores - top_score)
        probs = expo / jnp.sum(expo, axis=2, keepdims=True)
        probs_low = lax.optimization_barrier(probs.astype(jnp.bfloat16)).astype(jnp.float32)
        attended = jnp.einsum("gij,jd->igd", probs_low, value_f)
        delta = jnp.sum(grad_f * attended, axis=2)
        grad_probs = jnp.einsum("igd,jd->gij", grad_f, value_f)
        grad_scores = probs * (grad_probs - delta.T[:, :, None])
        scaled_low = lax.optimization_barrier((grad_scores * scaling).astype(jnp.bfloat16)).astype(jnp.float32)
        grad_query = jnp.einsum("gij,jd->igd", scaled_low, key_f).astype(jnp.bfloat16)
        grad_key = jnp.einsum("gij,igd->jd", scaled_low, query_f).astype(jnp.bfloat16)
        grad_value = jnp.einsum("gij,igd->jd", probs_low, grad_f).astype(jnp.bfloat16)
        return grad_query, grad_key, grad_value

    grad_query, grad_key, grad_value = jax.vmap(one_group, in_axes=(1, 1, 1, 1), out_axes=(1, 1, 1))(
        query_heads, key_heads, value_heads, grad_heads)
    return grad_query.reshape(length, -1), grad_key.reshape(length, -1), grad_value.reshape(length, -1)


def reference(tokens_x, queries, key_rows, out_grad, value_weight, doc_starts):
    def one_section(pieces):
        inputs, query_s, key_s, grad_s, weight_s, starts_s = pieces
        values = jnp.dot(inputs, weight_s, preferred_element_type=jnp.float32).astype(jnp.bfloat16)
        grad_query, grad_key, grad_value = attend(query_s, key_s, values, grad_s, starts_s)
        weight_grad = jnp.dot(inputs.T, grad_value, preferred_element_type=jnp.float32).astype(jnp.bfloat16)
        input_grad = jnp.dot(grad_value, weight_s.T, preferred_element_type=jnp.float32).astype(jnp.bfloat16)
        return grad_query, grad_key, weight_grad, input_grad

    query_grad, key_grad, weight_grad, input_grad = lax.map(
        one_section, (tokens_x, queries, key_rows, out_grad, value_weight, doc_starts))
    section_grad = jnp.concatenate([input_grad[1:], jnp.zeros_like(input_grad[:1])], axis=0)
    return (query_grad, key_grad, weight_grad, section_grad)
```

```python
import jax
import jax.numpy as jnp
from jax import lax
from jax.sharding import PartitionSpec as P

HD = 128


def from_behind(value, axis, steps):
    count = lax.axis_size(axis)
    first, last = (max(0, -steps), min(count, count - steps))
    return lax.ppermute(value, axis, [(source, source + steps) for source in range(first, last)])


def attend(queries, key_rows, values, out_grad, doc_starts):
    length = queries.shape[0]
    kv_heads = key_rows.shape[1] // HD
    groups = queries.shape[1] // (kv_heads * HD)
    scaling = HD ** (-0.5)
    row_index = lax.broadcasted_iota(jnp.int32, (length, length), 0)
    col_index = lax.broadcasted_iota(jnp.int32, (length, length), 1)
    allowed = (col_index <= row_index) & (col_index >= doc_starts[:, None])
    query_heads = queries.reshape(length, kv_heads, groups, HD)
    key_heads = key_rows.reshape(length, kv_heads, HD)
    value_heads = values.reshape(length, kv_heads, HD)
    grad_heads = out_grad.reshape(length, kv_heads, groups, HD)

    def one_group(query_g, key_g, value_g, grad_g):
        scores = (
            jnp.einsum("igd,jd->gij", query_g, key_g, preferred_element_type=jnp.float32) * scaling
        )
        scores = jnp.where(allowed[None], scores, -1e30)
        top_score = jnp.max(scores, axis=2, keepdims=True)
        expo = jnp.exp(scores - top_score)
        probs = expo / jnp.sum(expo, axis=2, keepdims=True)
        probs_low = probs.astype(jnp.bfloat16)
        attended = jnp.einsum("gij,jd->igd", probs_low, value_g, preferred_element_type=jnp.float32)
        delta = jnp.sum(grad_g.astype(jnp.float32) * attended, axis=2)
        grad_probs = jnp.einsum("igd,jd->gij", grad_g, value_g, preferred_element_type=jnp.float32)
        grad_scores = probs * (grad_probs - delta.T[:, :, None])
        scaled_low = (grad_scores * scaling).astype(jnp.bfloat16)
        grad_query = jnp.einsum(
            "gij,jd->igd", scaled_low, key_g, preferred_element_type=jnp.float32
        ).astype(jnp.bfloat16)
        grad_key = jnp.einsum(
            "gij,igd->jd", scaled_low, query_g, preferred_element_type=jnp.float32
        ).astype(jnp.bfloat16)
        grad_value = jnp.einsum(
            "gij,igd->jd", probs_low, grad_g, preferred_element_type=jnp.float32
        ).astype(jnp.bfloat16)
        return (grad_query, grad_key, grad_value)

    grad_query, grad_key, grad_value = jax.vmap(
        one_group, in_axes=(1, 1, 1, 1), out_axes=(1, 1, 1)
    )(query_heads, key_heads, value_heads, grad_heads)
    return (
        grad_query.reshape(length, -1),
        grad_key.reshape(length, -1),
        grad_value.reshape(length, -1),
    )


def sum_columns(terms, axis):
    count = lax.axis_size(axis)
    me = lax.axis_index(axis)
    width = terms.shape[1] // count
    total = lax.dynamic_slice_in_dim(terms, me * width, width, axis=1)
    for step in range(1, count):
        target = lax.rem(me + step, count)
        block = lax.dynamic_slice_in_dim(terms, target * width, width, axis=1)
        total = total + lax.ppermute(
            block, axis, [(source, (source + step) % count) for source in range(count)]
        )
    return total


def join_columns(block, axis):
    count = lax.axis_size(axis)
    me = lax.axis_index(axis)
    width = block.shape[1]
    whole = jnp.zeros((block.shape[0], width * count), block.dtype)
    whole = lax.dynamic_update_slice_in_dim(whole, block, me * width, axis=1)
    for step in range(1, count):
        origin = lax.rem(me + count - step, count)
        came = lax.ppermute(
            block, axis, [(source, (source + step) % count) for source in range(count)]
        )
        whole = lax.dynamic_update_slice_in_dim(whole, came, origin * width, axis=1)
    return whole


def shards(tokens_x, queries, key_rows, out_grad, value_weight, doc_starts):
    inputs = tokens_x[0]
    query_s = queries[0]
    key_s = key_rows[0]
    grad_s = out_grad[0]
    panel = value_weight[0]
    starts_s = doc_starts[0]
    terms = jnp.dot(inputs, panel, preferred_element_type=jnp.float32)
    values = sum_columns(terms, "tensor").astype(jnp.bfloat16)
    grad_query, grad_key, grad_value = attend(query_s, key_s, values, grad_s, starts_s)
    grad_all = join_columns(grad_value, "tensor")
    input_grad = lax.dot_general(
        grad_all, panel, (((1,), (1,)), ((), ())), preferred_element_type=jnp.float32
    ).astype(jnp.bfloat16)
    received = from_behind(input_grad, "pipe", -1)
    weight_grad = lax.dot_general(
        inputs, grad_all, (((0,), (0,)), ((), ())), preferred_element_type=jnp.float32
    ).astype(jnp.bfloat16)
    return (grad_query[None], grad_key[None], weight_grad[None], received[None])


def solution(mesh):
    placed = (
        P("pipe", None, "tensor"),
        P("pipe", None, "tensor"),
        P("pipe", None, "tensor"),
        P("pipe", None, "tensor"),
        P("pipe", "tensor", None),
        P("pipe", None),
    )
    return jax.shard_map(
        shards,
        mesh=mesh,
        in_specs=placed,
        out_specs=(
            P("pipe", None, "tensor"),
            P("pipe", None, "tensor"),
            P("pipe", "tensor", None),
            P("pipe", None, "tensor"),
        ),
        check_vma=False,
    )
```

```python
import functools
import math

import jax
import jax.numpy as jnp
from jax import lax
from jax.experimental import pallas as pl
from jax.experimental.pallas import tpu as pltpu
from jax.sharding import PartitionSpec as P

HD = 128
ROWS = 128
SCALING = HD ** (-0.5)
TO_EXP2 = SCALING * math.log2(math.e)


def from_behind(value, axis, steps):
    count = lax.axis_size(axis)
    first, last = (max(0, -steps), min(count, count - steps))
    return lax.ppermute(value, axis, [(source, source + steps) for source in range(first, last)])


def fill_bias(starts_ref, bias):
    @pl.when(pl.program_id(0) == 0)
    def _():
        token_j = lax.broadcasted_iota(jnp.int32, bias.shape, 0)
        token_i = lax.broadcasted_iota(jnp.int32, bias.shape, 1)
        allowed = (token_j <= token_i) & (token_j >= starts_ref[...])
        bias[...] = jnp.where(allowed, 0.0, -1e30)


def stacked(ref, rows, pair, together):
    columns = pl.ds(pl.multiple_of(pair * (together * HD), HD), together * HD)
    block = ref[rows, columns]
    return jnp.concatenate(
        [block[:, at * HD : (at + 1) * HD] for at in range(together)], axis=0
    )


def times(left, right, dims=((1,), (0,))):
    return lax.dot_general(left, right, (dims, ((), ())), preferred_element_type=jnp.float32)


def exponents(key_ref, query_h, bias, rows, reach, together):
    scores = times(key_ref[:reach, :], query_h, ((1,), (1,)))
    return scores * TO_EXP2 + jnp.concatenate([bias[:reach, rows]] * together, axis=1)


def softmax_kernel(
    together, starts_ref, query_ref, grad_ref, key_ref, out_ref, top_ref, inv_ref, bias, total
):
    fill_bias(starts_ref, bias)
    length = query_ref.shape[0]
    total[...] = jnp.zeros_like(total)

    @pl.loop(0, query_ref.shape[1] // (together * HD))
    def _(pair):
        for at in range(length // ROWS):
            reach = (at + 1) * ROWS
            rows = slice(at * ROWS, reach)
            query_h = stacked(query_ref, rows, pair, together)
            grad_h = stacked(grad_ref, rows, pair, together)
            power = exponents(key_ref, query_h, bias, rows, reach, together)
            top = jnp.max(power, axis=0, keepdims=True)
            expo = jnp.exp2(power - top)
            inverse = 1.0 / jnp.sum(expo, axis=0, keepdims=True)
            probs_low = (expo * inverse).astype(jnp.bfloat16)
            total[:reach, :] += times(probs_low, grad_h)
            top_ref[0, pair, at : at + 1, :] = top
            inv_ref[0, pair, at : at + 1, :] = inverse

    out_ref[...] = total[...].astype(out_ref.dtype)


def grads_kernel(
    together,
    starts_ref,
    query_ref,
    grad_ref,
    key_ref,
    value_ref,
    top_ref,
    inv_ref,
    grad_query_ref,
    grad_key_ref,
    bias,
    total,
    key_t,
):
    fill_bias(starts_ref, bias)
    length = query_ref.shape[0]
    total[...] = jnp.zeros_like(total)
    key_t[...] = key_ref[...].astype(jnp.float32).T.astype(key_t.dtype)

    @pl.loop(0, query_ref.shape[1] // (together * HD))
    def _(pair):
        for at in range(length // ROWS):
            reach = (at + 1) * ROWS
            rows = slice(at * ROWS, reach)
            query_h = stacked(query_ref, rows, pair, together)
            grad_h = stacked(grad_ref, rows, pair, together)
            power = exponents(key_ref, query_h, bias, rows, reach, together)
            top = top_ref[0, pair, at : at + 1, :]
            inverse = inv_ref[0, pair, at : at + 1, :]
            probs = jnp.exp2(power - top) * inverse
            probs_low = probs.astype(jnp.bfloat16).astype(jnp.float32)
            grad_probs = times(value_ref[:reach, :], grad_h, ((1,), (1,)))
            delta = jnp.sum(probs_low * grad_probs, axis=0, keepdims=True)
            scaled_low = (probs * (grad_probs - delta) * SCALING).astype(jnp.bfloat16)
            total[:reach, :] += times(scaled_low, query_h)
            grad_t = times(key_t[:, :reach], scaled_low)
            for head in range(together):
                columns = pl.ds(pl.multiple_of((pair * together + head) * HD, HD), HD)
                piece = grad_t[:, head * ROWS : (head + 1) * ROWS]
                grad_query_ref[rows, columns] = piece.T.astype(grad_query_ref.dtype)

    grad_key_ref[...] = total[...].astype(grad_key_ref.dtype)


def attention_calls(queries, key_rows):
    length = queries.shape[0]
    kv_heads = key_rows.shape[1] // HD
    width = queries.shape[1] // kv_heads
    groups = width // HD
    together = 2 if groups % 2 == 0 else 1
    starts_spec = pl.BlockSpec((1, length), lambda g: (0, 0))
    wide_spec = pl.BlockSpec((length, width), lambda g: (0, g))
    slim_spec = pl.BlockSpec((length, HD), lambda g: (0, g))
    stat_shape = (kv_heads, groups // together, length // ROWS, together * ROWS)
    stat_spec = pl.BlockSpec((1,) + stat_shape[1:], lambda g: (g, 0, 0, 0))
    stat = jax.ShapeDtypeStruct(stat_shape, jnp.float32)
    slim = jax.ShapeDtypeStruct(key_rows.shape, jnp.bfloat16)
    wide = jax.ShapeDtypeStruct(queries.shape, jnp.bfloat16)
    bias = pltpu.VMEM((length, length), jnp.float32)
    total = pltpu.VMEM((length, HD), jnp.float32)
    pairs = kv_heads * groups * length * length
    params = pltpu.CompilerParams(vmem_limit_bytes=32 * 2**20)
    softmax = pl.pallas_call(
        functools.partial(softmax_kernel, together),
        grid=(kv_heads,),
        in_specs=[starts_spec, wide_spec, wide_spec, slim_spec],
        out_specs=[slim_spec, stat_spec, stat_spec],
        out_shape=[slim, stat, stat],
        scratch_shapes=[bias, total],
        compiler_params=params,
        cost_estimate=pl.CostEstimate(
            flops=pairs * HD * 4, bytes_accessed=4 * queries.size, transcendentals=pairs
        ),
        name="softmax_value_grad",
    )
    grads = pl.pallas_call(
        functools.partial(grads_kernel, together),
        grid=(kv_heads,),
        in_specs=[starts_spec, wide_spec, wide_spec, slim_spec, slim_spec, stat_spec, stat_spec],
        out_specs=[wide_spec, slim_spec],
        out_shape=[wide, slim],
        scratch_shapes=[bias, total, pltpu.VMEM((HD, length), jnp.bfloat16)],
        compiler_params=params,
        cost_estimate=pl.CostEstimate(
            flops=pairs * HD * 8, bytes_accessed=6 * queries.size, transcendentals=pairs
        ),
        name="query_key_grad",
    )
    return softmax, grads


def sum_columns(terms, axis):
    count = lax.axis_size(axis)
    me = lax.axis_index(axis)
    width = terms.shape[1] // count
    total = lax.dynamic_slice_in_dim(terms, me * width, width, axis=1)
    for step in range(1, count):
        target = lax.rem(me + step, count)
        block = lax.dynamic_slice_in_dim(terms, target * width, width, axis=1)
        total = total + lax.ppermute(
            block, axis, [(source, (source + step) % count) for source in range(count)]
        )
    return total


def join_columns(block, axis):
    count = lax.axis_size(axis)
    me = lax.axis_index(axis)
    width = block.shape[1]
    whole = jnp.zeros((block.shape[0], width * count), block.dtype)
    whole = lax.dynamic_update_slice_in_dim(whole, block, me * width, axis=1)
    for step in range(1, count):
        origin = lax.rem(me + count - step, count)
        came = lax.ppermute(
            block, axis, [(source, (source + step) % count) for source in range(count)]
        )
        whole = lax.dynamic_update_slice_in_dim(whole, came, origin * width, axis=1)
    return whole


def shards(tokens_x, queries, key_rows, out_grad, value_weight, doc_starts):
    inputs = tokens_x[0]
    query_s = queries[0]
    key_s = key_rows[0]
    grad_s = out_grad[0]
    panel = value_weight[0]
    softmax, grads = attention_calls(query_s, key_s)
    grad_value, top, inverse = softmax(doc_starts, query_s, grad_s, key_s)
    grad_value, inputs = lax.optimization_barrier((grad_value, inputs))
    grad_all = join_columns(grad_value, "tensor")
    terms = jnp.dot(inputs, panel, preferred_element_type=jnp.float32)
    values = sum_columns(terms, "tensor").astype(jnp.bfloat16)
    input_grad = lax.dot_general(
        grad_all, panel, (((1,), (1,)), ((), ())), preferred_element_type=jnp.float32
    ).astype(jnp.bfloat16)
    received = from_behind(input_grad, "pipe", -1)
    grad_query, grad_key = grads(doc_starts, query_s, grad_s, key_s, values, top, inverse)
    weight_grad = lax.dot_general(
        inputs, grad_all, (((0,), (0,)), ((), ())), preferred_element_type=jnp.float32
    ).astype(jnp.bfloat16)
    return (grad_query[None], grad_key[None], weight_grad[None], received[None])


def solution(mesh):
    placed = (
        P("pipe", None, "tensor"),
        P("pipe", None, "tensor"),
        P("pipe", None, "tensor"),
        P("pipe", None, "tensor"),
        P("pipe", "tensor", None),
        P("pipe", None),
    )
    return jax.shard_map(
        shards,
        mesh=mesh,
        in_specs=placed,
        out_specs=(
            P("pipe", None, "tensor"),
            P("pipe", None, "tensor"),
            P("pipe", "tensor", None),
            P("pipe", None, "tensor"),
        ),
        check_vma=False,
    )
```

```python
import functools
import math

import jax
import jax.numpy as jnp
from jax import lax
from jax.experimental import pallas as pl
from jax.experimental.pallas import tpu as pltpu
from jax.sharding import PartitionSpec as P

HD = 128
ROWS = 128
PARTS = 2
SCALING = HD ** (-0.5)
TO_EXP2 = SCALING * math.log2(math.e)


def from_behind(value, axis, steps):
    count = lax.axis_size(axis)
    first, last = (max(0, -steps), min(count, count - steps))
    return lax.ppermute(value, axis, [(source, source + steps) for source in range(first, last)])


def fill_bias(starts_ref, bias):
    @pl.when(pl.program_id(0) == 0)
    def _():
        token_j = lax.broadcasted_iota(jnp.int32, bias.shape, 0)
        token_i = lax.broadcasted_iota(jnp.int32, bias.shape, 1)
        allowed = (token_j <= token_i) & (token_j >= starts_ref[...])
        bias[...] = jnp.where(allowed, 0.0, -1e30)


def stacked(ref, rows, pair, together):
    columns = pl.ds(pl.multiple_of(pair * (together * HD), HD), together * HD)
    block = ref[rows, columns]
    return jnp.concatenate(
        [block[:, at * HD : (at + 1) * HD] for at in range(together)], axis=0
    )


def times(left, right, dims=((1,), (0,))):
    return lax.dot_general(left, right, (dims, ((), ())), preferred_element_type=jnp.float32)


def exponents(key_ref, query_h, bias, rows, reach, together):
    scores = times(key_ref[:reach, :], query_h, ((1,), (1,)))
    return scores * TO_EXP2 + jnp.concatenate([bias[:reach, rows]] * together, axis=1)


def softmax_kernel(
    together, starts_ref, query_ref, grad_ref, key_ref, out_ref, top_ref, inv_ref, bias, total
):
    fill_bias(starts_ref, bias)
    length = query_ref.shape[0]
    total[...] = jnp.zeros_like(total)

    pairs = query_ref.shape[1] // (together * HD)
    unroll = math.gcd(pairs, 6)

    @pl.loop(0, pairs, step=unroll)
    def _(first):
        for at, pair in [(a, first + u) for a in range(length // ROWS) for u in range(unroll)]:
            reach = (at + 1) * ROWS
            rows = slice(at * ROWS, reach)
            query_h = stacked(query_ref, rows, pair, together)
            grad_h = stacked(grad_ref, rows, pair, together)
            power = exponents(key_ref, query_h, bias, rows, reach, together)
            top = jnp.max(power, axis=0, keepdims=True)
            expo = jnp.exp2(power - top)
            inverse = 1.0 / jnp.sum(expo, axis=0, keepdims=True)
            probs_low = (expo * inverse).astype(jnp.bfloat16)
            total[:reach, :] += times(probs_low, grad_h)
            top_ref[0, pair, at : at + 1, :] = top
            inv_ref[0, pair, at : at + 1, :] = inverse

    out_ref[...] = total[...].astype(out_ref.dtype)


def grads_kernel(
    together,
    starts_ref,
    query_ref,
    grad_ref,
    key_ref,
    value_ref,
    top_ref,
    inv_ref,
    grad_query_ref,
    grad_key_ref,
    bias,
    total,
    key_t,
):
    fill_bias(starts_ref, bias)
    length = query_ref.shape[0]
    total[...] = jnp.zeros_like(total)
    key_t[...] = key_ref[...].astype(jnp.float32).T.astype(key_t.dtype)

    pairs = query_ref.shape[1] // (together * HD)
    unroll = math.gcd(pairs, 6)

    @pl.loop(0, pairs, step=unroll)
    def _(first):
        for at, pair in [(a, first + u) for a in range(length // ROWS) for u in range(unroll)]:
            reach = (at + 1) * ROWS
            rows = slice(at * ROWS, reach)
            query_h = stacked(query_ref, rows, pair, together)
            grad_h = stacked(grad_ref, rows, pair, together)
            power = exponents(key_ref, query_h, bias, rows, reach, together)
            top = top_ref[0, pair, at : at + 1, :]
            inverse = inv_ref[0, pair, at : at + 1, :]
            probs = jnp.exp2(power - top) * inverse
            probs_low = probs.astype(jnp.bfloat16).astype(jnp.float32)
            grad_probs = times(value_ref[:reach, :], grad_h, ((1,), (1,)))
            delta = jnp.sum(probs_low * grad_probs, axis=0, keepdims=True)
            scaled_low = (probs * (grad_probs - delta) * SCALING).astype(jnp.bfloat16)
            total[:reach, :] += times(scaled_low, query_h)
            grad_t = times(key_t[:, :reach], scaled_low)
            for head in range(together):
                columns = pl.ds(pl.multiple_of((pair * together + head) * HD, HD), HD)
                piece = grad_t[:, head * ROWS : (head + 1) * ROWS]
                grad_query_ref[rows, columns] = piece.T.astype(grad_query_ref.dtype)

    grad_key_ref[...] = total[...].astype(grad_key_ref.dtype)


def attention_calls(queries, key_rows):
    length = queries.shape[0]
    kv_heads = key_rows.shape[1] // HD
    width = queries.shape[1] // kv_heads
    groups = width // HD
    together = 2 if groups % 2 == 0 else 1
    starts_spec = pl.BlockSpec((1, length), lambda g: (0, 0))
    wide_spec = pl.BlockSpec((length, width), lambda g: (0, g))
    slim_spec = pl.BlockSpec((length, HD), lambda g: (0, g))
    stat_shape = (kv_heads, groups // together, length // ROWS, together * ROWS)
    stat_spec = pl.BlockSpec((1,) + stat_shape[1:], lambda g: (g, 0, 0, 0))
    stat = jax.ShapeDtypeStruct(stat_shape, jnp.float32)
    slim = jax.ShapeDtypeStruct(key_rows.shape, jnp.bfloat16)
    wide = jax.ShapeDtypeStruct(queries.shape, jnp.bfloat16)
    bias = pltpu.VMEM((length, length), jnp.float32)
    total = pltpu.VMEM((length, HD), jnp.float32)
    pairs = kv_heads * groups * length * length
    params = pltpu.CompilerParams(vmem_limit_bytes=56 * 2**20)
    softmax = pl.pallas_call(
        functools.partial(softmax_kernel, together),
        grid=(kv_heads,),
        in_specs=[starts_spec, wide_spec, wide_spec, slim_spec],
        out_specs=[slim_spec, stat_spec, stat_spec],
        out_shape=[slim, stat, stat],
        scratch_shapes=[bias, total],
        compiler_params=params,
        cost_estimate=pl.CostEstimate(
            flops=pairs * HD * 4, bytes_accessed=4 * queries.size, transcendentals=pairs
        ),
        name="softmax_value_grad",
    )
    grads = pl.pallas_call(
        functools.partial(grads_kernel, together),
        grid=(kv_heads,),
        in_specs=[starts_spec, wide_spec, wide_spec, slim_spec, slim_spec, stat_spec, stat_spec],
        out_specs=[wide_spec, slim_spec],
        out_shape=[wide, slim],
        scratch_shapes=[bias, total, pltpu.VMEM((HD, length), jnp.bfloat16)],
        compiler_params=params,
        cost_estimate=pl.CostEstimate(
            flops=pairs * HD * 8, bytes_accessed=6 * queries.size, transcendentals=pairs
        ),
        name="query_key_grad",
    )
    return softmax, grads


def sum_columns(terms, axis):
    count = lax.axis_size(axis)
    me = lax.axis_index(axis)
    width = terms.shape[1] // count
    total = lax.dynamic_slice_in_dim(terms, me * width, width, axis=1)
    for step in range(1, count):
        target = lax.rem(me + step, count)
        block = lax.dynamic_slice_in_dim(terms, target * width, width, axis=1)
        total = total + lax.ppermute(
            block, axis, [(source, (source + step) % count) for source in range(count)]
        )
    return total


def join_columns(block, axis):
    count = lax.axis_size(axis)
    me = lax.axis_index(axis)
    width = block.shape[1]
    whole = jnp.zeros((block.shape[0], width * count), block.dtype)
    whole = lax.dynamic_update_slice_in_dim(whole, block, me * width, axis=1)
    for step in range(1, count):
        origin = lax.rem(me + count - step, count)
        came = lax.ppermute(
            block, axis, [(source, (source + step) % count) for source in range(count)]
        )
        whole = lax.dynamic_update_slice_in_dim(whole, came, origin * width, axis=1)
    return whole


def shards(tokens_x, queries, key_rows, out_grad, value_weight, doc_starts):
    inputs = tokens_x[0]
    query_s = queries[0]
    key_s = key_rows[0]
    grad_s = out_grad[0]
    panel = value_weight[0]
    softmax, grads = attention_calls(query_s, key_s)
    grad_value, top, inverse = softmax(doc_starts, query_s, grad_s, key_s)
    grad_value, inputs = lax.optimization_barrier((grad_value, inputs))
    grad_all = join_columns(grad_value, "tensor")
    terms = jnp.dot(inputs, panel, preferred_element_type=jnp.float32)
    grad_all, terms = lax.optimization_barrier((grad_all, terms))
    values = sum_columns(terms, "tensor").astype(jnp.bfloat16)
    came = []
    for part in jnp.split(panel, PARTS, axis=0):
        input_grad = lax.dot_general(
            grad_all, part, (((1,), (1,)), ((), ())), preferred_element_type=jnp.float32
        ).astype(jnp.bfloat16)
        came.append(from_behind(input_grad, "pipe", -1))
    received = jnp.concatenate(came, axis=1)
    grad_query, grad_key = grads(doc_starts, query_s, grad_s, key_s, values, top, inverse)
    weight_grad = lax.dot_general(
        inputs, grad_all, (((0,), (0,)), ((), ())), preferred_element_type=jnp.float32
    ).astype(jnp.bfloat16)
    return (grad_query[None], grad_key[None], weight_grad[None], received[None])


def solution(mesh):
    placed = (
        P("pipe", None, "tensor"),
        P("pipe", None, "tensor"),
        P("pipe", None, "tensor"),
        P("pipe", None, "tensor"),
        P("pipe", "tensor", None),
        P("pipe", None),
    )
    return jax.shard_map(
        shards,
        mesh=mesh,
        in_specs=placed,
        out_specs=(
            P("pipe", None, "tensor"),
            P("pipe", None, "tensor"),
            P("pipe", "tensor", None),
            P("pipe", None, "tensor"),
        ),
        check_vma=False,
    )
```
